32 devices in a mesh: section: 4 (over x, core), expert: 8 (over z, y).
Axes of the slice: x: 2, y: 2, z: 4, core: 2. Of those that a mesh axis runs over, the one named last changes fastest.
Arguments:
- sent_acts: bfloat16 [4, 512, 2048], P('section', 'expert'), may hold values from -6 to 6
- stash: bfloat16 [4, 512, 2048], P('section', 'expert'), may hold values from -6 to 6
- cotangents: bfloat16 [4, 512, 2048], P('section', 'expert'), may hold values from -6 to 6
- norm_gain: bfloat16 [4, 2048], P('section'), may hold values from 0.5 to 1.5
- w_gate: bfloat16 [4, 16, 2048, 768], P('section', 'expert'), may hold values from -0.125 to 0.125
- w_up: bfloat16 [4, 16, 2048, 768], P('section', 'expert'), may hold values from -0.125 to 0.125
- w_down: bfloat16 [4, 16, 768, 2048], P('section', 'expert'), may hold values from -0.21875 to 0.21875
- routes_next: int32 [4, 512, 8], P('section', 'expert'), may hold values from 0 to 15, all different within a row; in each aligned block of 64 rows (0 to 63, 64 to 127, ..., all dimensions but the last counted through in order) at most 48 rows name the same one
- gates_next: bfloat16 [4, 512, 8], P('section', 'expert'), may hold values from 0.049804688 to 0.5
- routes_prev: int32 [4, 512, 8], P('section', 'expert'), may hold values from 0 to 15, all different within a row; in each aligned block of 64 rows (0 to 63, 64 to 127, ..., all dimensions but the last counted through in order) at most 48 rows name the same one
- gates_prev: bfloat16 [4, 512, 8], P('section', 'expert'), may hold values from 0.049804688 to 0.5
Outputs:
- fwd_out: bfloat16 [4, 512, 2048], P('section', 'expert')
- bwd_out: bfloat16 [4, 512, 2048], P('section', 'expert')
- gate_grad: bfloat16 [4, 512, 8], P('section', 'expert')
- grad_w_gate: bfloat16 [4, 16, 2048, 768], P('section', 'expert')
- grad_w_up: bfloat16 [4, 16, 2048, 768], P('section', 'expert')
- grad_w_down: bfloat16 [4, 16, 768, 2048], P('section', 'expert')
The draws below stay inside these ranges and needn't reach their ends.
Inputs may be any that keep to these rules, and one draw needn't show every extreme that they name: `routes_next`: each row names 8 different experts. At most 48 of the 64 tokens of one device choose one expert, and in some device's tokens some expert is chosen by exactly 48. `routes_prev`: each row names 8 different experts. At most 48 of the 64 tokens of one device choose one expert, and in some device's tokens some expert is chosen by exactly 48.
All inputs are finite; a program needn't handle non-finite values.
Results may differ from the reference program's by a relative error of at most 0.008.
Values may be sent and summed in bfloat16 or wider, within the bound.
A program may use at most 128 MiB of HBM per device.

```python
import math
import jax
import jax.numpy as jnp
import numpy as np
from jax import lax

D = 2048
FF = 768
EXPERTS = 16
TOP = 8
TOK_DEV = 64
SECTIONS = 4
TOKENS = 512
CAP = 48
N_EXPERT = 8


def level_of(own_key, dims, split, low, top_value):
    def one(dim, blocks):
        heights = jax.random.uniform(jax.random.fold_in(jax.random.fold_in(own_key, 6), dim), (blocks,), jnp.float32, low / len(split), top_value / len(split))
        return jnp.repeat(jnp.exp(heights), dims[dim] // blocks).reshape((-1,) + (1,) * (len(dims) - dim - 1))

    gain = one(*split[0])
    for cut in split[1:]:
        gain = gain * one(*cut)
    return gain


def routed_block(stream_key, own, number, rows, number_of, top, limit, lean):
    ranking = jax.random.permutation(stream_key, number_of)
    packed, common = portions_of(number_of, rows * top, limit, lean, True), portions_of(number_of, rows * top, limit, lean, False)
    places = jnp.arange(number_of)

    def named(sizes, offset_by):
        used = int((sizes > 0).sum())
        fixed = max(1, used // 4)
        shifted = fixed + (places - fixed + offset_by * (used - fixed)) % max(1, number_of - fixed)
        return jnp.zeros((number_of,), jnp.int32).at[ranking[jnp.where(places < fixed, places, shifted)]].set(jnp.asarray(sizes, jnp.int32))

    sizes = jnp.where(number % 4 == 0, named(packed, number // 4), named(common, number - number // 4 - 1))
    mixed = jax.random.permutation(jax.random.fold_in(own, 3), number_of)
    donor, taker = mixed[0:number_of // 2 * 2:2], mixed[1:number_of // 2 * 2:2]
    slack = jnp.minimum(sizes[donor] - 1, limit - sizes[taker]) // 2
    slack = jnp.where((donor == ranking[0]) | (taker == ranking[0]) | (sizes[taker] == 0), 0, jnp.maximum(slack, 0))
    shifted = jax.random.randint(jax.random.fold_in(own, 4), (number_of // 2,), 0, 1 << 20) % (slack + 1)
    sizes = sizes.at[donor].add(-shifted).at[taker].add(shifted)
    items = jnp.searchsorted(jnp.cumsum(sizes), jnp.arange(rows * top), side="right").astype(jnp.int32)
    table = items.reshape(top, rows).T
    table = table[jax.random.permutation(jax.random.fold_in(own, 1), rows)]
    offset_by = jax.random.randint(jax.random.fold_in(own, 2), (rows, 1), 0, top)
    return jnp.take_along_axis(table, (jnp.arange(top)[None, :] + offset_by) % top, axis=1)


def portions_of(number_of, total, reach, skew, full):
    loads = [(1 << 20) // math.isqrt(standing ** skew) + 1 for standing in range(1, number_of + 1)]
    largest = reach if full else min(reach, max(-(-total // number_of), total * loads[0] // sum(loads)))
    least = 1 if total - largest >= number_of - 1 else 0
    given, surplus = [largest] + [least] * (number_of - 1), total - largest - least * (number_of - 1)
    while surplus > 0:
        movable = [i for i in range(1, number_of) if given[i] < largest] or [i for i in range(1, number_of) if given[i] < reach]
        mass, left = sum([loads[i] for i in movable]), surplus
        for i in movable:
            more = min(reach - given[i], max(1, left * loads[i] // mass), surplus)
            given[i] = given[i] + more
            surplus = surplus - more
    return np.array(given)


def noise(own_key, shape, spread, bound, cuts=(), held_as=jnp.bfloat16):
    entries = jax.random.normal(own_key, shape, jnp.float32) * spread
    if len(cuts) > 0:
        entries = level_of(own_key, shape, cuts, -0.22, 0.18) * entries
    return jnp.clip(entries, min=-bound, max=bound).astype(held_as)


def setup_inputs(seed: int = 0) -> dict:
    key_list = jax.random.split(jax.random.key(seed), 12)
    sent_acts = noise(key_list[0], (SECTIONS, TOKENS, D), 1.0, 6.0, ((0, 4), (1, 8)))
    stash = noise(key_list[1], (SECTIONS, TOKENS, D), 1.0, 6.0, ((0, 4), (1, 8)))
    cotangents = noise(key_list[2], (SECTIONS, TOKENS, D), 1.0, 6.0, ((0, 4), (1, 8)))
    norm_gain = jnp.clip(1.0 + 0.1 * jax.random.normal(key_list[3], (SECTIONS, D), jnp.float32), 0.5, 1.5).astype(jnp.bfloat16)
    w_gate = noise(key_list[4], (SECTIONS, EXPERTS, D, FF), D ** -0.5, 0.125, ((0, 4), (1, 8)))
    w_up = noise(key_list[5], (SECTIONS, EXPERTS, D, FF), D ** -0.5, 0.125, ((0, 4), (1, 8)))
    w_down = noise(key_list[6], (SECTIONS, EXPERTS, FF, D), FF ** -0.5, 0.21875, ((0, 4), (1, 8)))
    routes_next_keys = jax.random.split(jax.random.fold_in(key_list[7], 1), SECTIONS * TOKENS // TOK_DEV)
    routes_next_turns = jax.random.permutation(jax.random.fold_in(key_list[7], 3), SECTIONS * TOKENS // TOK_DEV)
    routes_next = jax.vmap(lambda own, number: routed_block(jax.random.fold_in(key_list[7], 2), own, number, TOK_DEV, EXPERTS, TOP, CAP, 2))(routes_next_keys, routes_next_turns).reshape((SECTIONS, TOKENS, TOP))
    gates_next = jnp.clip(jnp.exp(math.log(0.5) - 2.306499 * jax.random.uniform(key_list[8], (SECTIONS, TOKENS, TOP), jnp.float32) ** level_of(key_list[8], (SECTIONS, TOKENS, TOP), ((0, 4), (1, 8)), -0.2, 0.2)), 0.049804688, 0.5).astype(jnp.bfloat16)
    routes_prev_keys = jax.random.split(jax.random.fold_in(key_list[9], 1), SECTIONS * TOKENS // TOK_DEV)
    routes_prev_turns = jax.random.permutation(jax.random.fold_in(key_list[9], 3), SECTIONS * TOKENS // TOK_DEV)
    routes_prev = jax.vmap(lambda own, number: routed_block(jax.random.fold_in(key_list[9], 2), own, number, TOK_DEV, EXPERTS, TOP, CAP, 2))(routes_prev_keys, routes_prev_turns).reshape((SECTIONS, TOKENS, TOP))
    gates_prev = jnp.clip(jnp.exp(math.log(0.5) - 2.306499 * jax.random.uniform(key_list[10], (SECTIONS, TOKENS, TOP), jnp.float32) ** level_of(key_list[10], (SECTIONS, TOKENS, TOP), ((0, 4), (1, 8)), -0.2, 0.2)), 0.049804688, 0.5).astype(jnp.bfloat16)
    return {"sent_acts": sent_acts, "stash": stash, "cotangents": cotangents, "norm_gain": norm_gain, "w_gate": w_gate, "w_up": w_up, "w_down": w_down, "routes_next": routes_next, "gates_next": gates_next, "routes_prev": routes_prev, "gates_prev": gates_prev}


EPS = 1e-06

def apply_rms_norm(rows, norm_scale_weight):
    value_entries = rows.astype(jnp.float32)
    inverse_root_scale = lax.rsqrt(lax.optimization_barrier(jnp.mean(value_entries * value_entries, axis=-1, keepdims=True)) + EPS)
    unit_rows = value_entries * inverse_root_scale
    normalized_rows = (unit_rows * norm_scale_weight.astype(jnp.float32)).astype(jnp.bfloat16)
    return (normalized_rows, unit_rows, inverse_root_scale)

def place_slots(routes):
    flat = routes.reshape(-1).astype(jnp.int32)
    onehot = (flat[:, None] == jnp.arange(EXPERTS, dtype=jnp.int32)[None, :]).astype(jnp.int32)
    before = jnp.cumsum(onehot, axis=0) - onehot
    slot = lax.optimization_barrier(jnp.sum(before * onehot, axis=1)).astype(jnp.int32)
    return (flat, slot)

def dispatch(rows, flat, slot):

    def one_block(block_rows, block_flat, block_slot):
        buffer = jnp.zeros((EXPERTS, CAP) + block_rows.shape[1:], block_rows.dtype)
        return buffer.at[block_flat, block_slot].set(block_rows)
    buffers = jax.vmap(one_block)(rows, flat, slot)
    return jnp.swapaxes(buffers, 0, 1)

def collect(buffers, flat, slot):
    per_block = jnp.swapaxes(buffers, 0, 1)
    return jax.vmap(lambda block, block_flat, block_slot: block[block_flat, block_slot])(per_block, flat, slot)

def expert_forward(args):
    rows, weight_gate, weight_up, weight_down = args
    pre_gate = jnp.dot(rows, weight_gate, preferred_element_type=jnp.float32)
    pre_up = jnp.dot(rows, weight_up, preferred_element_type=jnp.float32)
    hidden = (jax.nn.silu(pre_gate) * pre_up).astype(jnp.bfloat16)
    return jnp.dot(hidden, weight_down, preferred_element_type=jnp.float32).astype(jnp.bfloat16)

def expert_backward(args):
    rows, out_grad, weight_gate, weight_up, weight_down = args
    pre_gate = jnp.dot(rows, weight_gate, preferred_element_type=jnp.float32)
    pre_up = jnp.dot(rows, weight_up, preferred_element_type=jnp.float32)
    sigma = jax.nn.sigmoid(pre_gate)
    active = pre_gate * sigma
    hidden = (active * pre_up).astype(jnp.bfloat16)
    expert_out = jnp.dot(hidden, weight_down, preferred_element_type=jnp.float32).astype(jnp.bfloat16)
    d_hidden = jnp.dot(out_grad, weight_down.T, preferred_element_type=jnp.float32)
    d_gate = (d_hidden * pre_up * sigma * (1.0 + pre_gate * (1.0 - sigma))).astype(jnp.bfloat16)
    d_up = (d_hidden * active).astype(jnp.bfloat16)
    row_grad = (jnp.dot(d_gate, weight_gate.T, preferred_element_type=jnp.float32) + jnp.dot(d_up, weight_up.T, preferred_element_type=jnp.float32)).astype(jnp.bfloat16)
    grad_gate = jnp.dot(rows.T, d_gate, preferred_element_type=jnp.float32).astype(jnp.bfloat16)
    grad_up = jnp.dot(rows.T, d_up, preferred_element_type=jnp.float32).astype(jnp.bfloat16)
    grad_down = jnp.dot(hidden.T, out_grad, preferred_element_type=jnp.float32).astype(jnp.bfloat16)
    return (expert_out, row_grad, grad_gate, grad_up, grad_down)

def reference(sent_acts, stash, cotangents, norm_gain, w_gate, w_up, w_down, routes_next, gates_next, routes_prev, gates_prev):
    fwd_list, bwd_list, gate_list, wg_list, wu_list, wd_list = ([], [], [], [], [], [])
    for section_index in range(SECTIONS):
        norm_scale_weight = norm_gain[section_index]
        weight_gate, weight_up, weight_down = (w_gate[section_index], w_up[section_index], w_down[section_index])
        arrived = sent_acts[(section_index - 1) % SECTIONS]
        normalized_rows, _, _ = apply_rms_norm(arrived, norm_scale_weight)
        flat, slot = jax.vmap(place_slots)(routes_next[section_index].reshape(N_EXPERT, TOK_DEV, TOP))
        rows = jnp.repeat(normalized_rows, TOP, axis=0).reshape(N_EXPERT, TOK_DEV * TOP, D)
        buffers = dispatch(rows, flat, slot).reshape(EXPERTS, N_EXPERT * CAP, D)
        outputs = lax.map(expert_forward, (buffers, weight_gate, weight_up, weight_down))
        picked = collect(outputs.reshape(EXPERTS, N_EXPERT, CAP, D), flat, slot).reshape(TOKENS, TOP, D)
        mixed = lax.optimization_barrier(jnp.sum(gates_next[section_index].astype(jnp.float32)[..., None] * picked.astype(jnp.float32), axis=1))
        fwd_list.append((arrived.astype(jnp.float32) + mixed).astype(jnp.bfloat16))
        received_rows = cotangents[(section_index + 1) % SECTIONS]
        previous_normalized_rows, unit_rows, inverse_root_scale = apply_rms_norm(stash[section_index], norm_scale_weight)
        flat_prev, slot_prev = jax.vmap(place_slots)(routes_prev[section_index].reshape(N_EXPERT, TOK_DEV, TOP))
        rows_prev = jnp.repeat(previous_normalized_rows, TOP, axis=0).reshape(N_EXPERT, TOK_DEV * TOP, D)
        out_grad = (gates_prev[section_index].astype(jnp.float32)[..., None] * received_rows.astype(jnp.float32)[:, None, :]).astype(jnp.bfloat16)
        out_grad = out_grad.reshape(N_EXPERT, TOK_DEV * TOP, D)
        row_buffers = dispatch(rows_prev, flat_prev, slot_prev).reshape(EXPERTS, N_EXPERT * CAP, D)
        grad_buffers = dispatch(out_grad, flat_prev, slot_prev).reshape(EXPERTS, N_EXPERT * CAP, D)
        expert_out, row_grad, grad_gate, grad_up, grad_down = lax.map(expert_backward, (row_buffers, grad_buffers, weight_gate, weight_up, weight_down))
        out_pick = collect(expert_out.reshape(EXPERTS, N_EXPERT, CAP, D), flat_prev, slot_prev).reshape(TOKENS, TOP, D)
        selected_gradient = collect(row_grad.reshape(EXPERTS, N_EXPERT, CAP, D), flat_prev, slot_prev).reshape(TOKENS, TOP, D)
        gate_list.append(lax.optimization_barrier(jnp.sum(out_pick.astype(jnp.float32) * received_rows.astype(jnp.float32)[:, None, :], axis=-1)).astype(jnp.bfloat16))
        normalized_gradient = lax.optimization_barrier(jnp.sum(selected_gradient.astype(jnp.float32), axis=1)) * norm_scale_weight.astype(jnp.float32)
        backward_result = received_rows.astype(jnp.float32) + inverse_root_scale * (normalized_gradient - unit_rows * lax.optimization_barrier(jnp.mean(normalized_gradient * unit_rows, axis=-1, keepdims=True)))
        bwd_list.append(backward_result.astype(jnp.bfloat16))
        wg_list.append(grad_gate)
        wu_list.append(grad_up)
        wd_list.append(grad_down)
    return (jnp.stack(fwd_list), jnp.stack(bwd_list), jnp.stack(gate_list), jnp.stack(wg_list), jnp.stack(wu_list), jnp.stack(wd_list))
```

```python
import functools

import jax
import jax.numpy as jnp
from jax import lax
from jax.experimental import pallas as pl
from jax.experimental.pallas import tpu as pltpu
from jax.sharding import PartitionSpec as P

EPS = 1e-06
F32 = jnp.float32
BF16 = jnp.bfloat16
LANES = 128
GROUP = 16
CHUNKS = 2
PREV, COT, NEXT = 0, 1, 2
ROW, MIX = 0, 1
VMEM = pl.BlockSpec(memory_space=pltpu.VMEM)
ANY = pl.BlockSpec(memory_space=pl.ANY)
VMEM_LIMIT = 61 * 2**20


class Ring:
    def __init__(self, sections, owners):
        bits = owners.bit_length() - 1
        self.n = owners
        self.half = owners // 2
        self.nz = 1 << ((bits + 1) // 2)
        self.ny = owners // self.nz
        self.section = lax.axis_index("section")
        self.sections = sections
        self.me = lax.axis_index("expert")
        z, y = self.me // self.ny, self.me % self.ny
        self.place = y * self.nz + z + (y % 2) * (self.nz - 1 - 2 * z)
        self.sides = (self.device(1), self.device(-1))

    def device(self, offset):
        p = (self.place + offset + self.n) % self.n
        y, r = p // self.nz, p % self.nz
        return (self.section, (r + (y % 2) * (self.nz - 1 - 2 * r)) * self.ny + y)

    def shifted(self, by):
        return ((self.section + by + self.sections) % self.sections, self.me)

    def slot(self, offset):
        offset = (offset + self.n) % self.n
        if offset > self.half:
            return 2 * (self.n - offset) - 1
        return 2 * offset - (offset == self.half)

    def greet(self):
        barrier = pltpu.get_barrier_semaphore()
        targets = [self.device(r) for r in range(1, self.n)]
        targets += [self.shifted(1), self.shifted(-1)]
        for target in targets:
            pl.semaphore_signal(
                barrier, inc=1, device_id=target, device_id_type=pl.DeviceIdType.MESH
            )
        return lambda: pl.semaphore_wait(barrier, len(targets))


def send(src, dst, send_sem, recv_sem, device):
    return pltpu.make_async_remote_copy(
        src_ref=src,
        dst_ref=dst,
        send_sem=send_sem,
        recv_sem=recv_sem,
        device_id=device,
        device_id_type=pl.DeviceIdType.MESH,
    )


def scale_of(values):
    return lax.rsqrt(jnp.mean(values * values, axis=-1, keepdims=True) + EPS)


def dot(a, b, ca, cb):
    return lax.dot_general(a, b, (((ca,), (cb,)), ((), ())), preferred_element_type=F32)


def flat(ref):
    value = ref[...]
    return value.reshape(-1, value.shape[-1])


def tile_of(size):
    return 256 if size % 256 == 0 else LANES


def span(i, size):
    return pl.ds(pl.multiple_of(i * size, size), size)


def eye(size):
    shape = (size, size)
    row, col = (lax.broadcasted_iota(jnp.int32, shape, d) for d in range(2))
    return (row == col).astype(BF16)


def run(count, body, actions=()):
    table = {}
    for n, action in enumerate(actions):
        table.setdefault((2 * n + 1) * count // (2 * len(actions)), []).append(action)

    @pl.loop(0, count)
    def _(i):
        for at, group in table.items():
            @pl.when(i == at)
            def _():
                for action in group:
                    action()
        body(i)


def tick_kernel(
    sections, owners,
    act_ref, stash_ref, cot_ref, gain_ref,
    routes_next_ref, choice_next_ref, routes_prev_ref, choice_prev_ref,
    wg_hbm, wu_hbm, wd_hbm,
    fwd_ref, bwd_ref, gate_grad_ref, wg, wu, wd,
    arrived_ref, prev_ref, cots_ref, next_ref, row_ref, part_ref, arriving,
    gates_ref, products_ref, returned_ref, weight_ref, sums,
    pre_gate, pre_up, d_gate, d_up, gated, hidden_ref,
    shift_send, shift_recv, gate_send, gate_recv, product_send, product_recv,
    gather_send, gather_recv, reduce_send, reduce_recv, weight_sem,
):
    ring = Ring(sections, owners)
    half = ring.half
    tokens, width = stash_ref.shape
    local, _, units = wg.shape
    experts = local * owners
    chunk = width // CHUNKS
    loads = [
        pltpu.make_async_copy(h, v, weight_sem.at[i])
        for i, (h, v) in enumerate(((wg_hbm, wg), (wu_hbm, wu), (wd_hbm, wd)))
    ]
    for copy in loads:
        copy.start()
    met = ring.greet()

    def normalize(source, target):
        @pl.loop(0, tokens // GROUP)
        def _(i):
            rows = span(i, GROUP)
            values = source[rows, :].astype(F32)
            target[0, rows, :] = (values * scale_of(values) * gain_ref[...].astype(F32)).astype(BF16)

    def dense_gates():
        lane = lax.broadcasted_iota(jnp.int32, (LANES, tokens), 0)
        total = jnp.zeros((LANES, tokens), F32)
        for base, routes, gates in (
            (0, routes_next_ref, choice_next_ref), (experts, routes_prev_ref, choice_prev_ref)
        ):
            names, values = routes[...] + base, gates[...].astype(F32)
            for k in range(names.shape[0]):
                total += jnp.where(names[k : k + 1] == lane, values[k : k + 1], 0.0)
        gates_ref[0] = dot(eye(tokens), total.astype(BF16), 1, 1).astype(BF16)

    buffers, parts = (prev_ref, cots_ref, next_ref), (row_ref, part_ref)
    ways = ((0, 1), (1, -1))

    def columns(c, d, cut):
        return pl.ds(c * chunk + d * (chunk // 2), chunk // 2) if cut else pl.ds(c * chunk, chunk)

    def gather(t, c, k):
        copies = []
        for d, way in ways:
            cols = columns(c, d, k == half - 1)
            copies.append(send(
                buffers[t].at[ring.slot(-way * k), :, cols],
                buffers[t].at[ring.slot(-way * (k + 1)), :, cols],
                gather_send.at[t, c, d, k], gather_recv.at[t, c, d, k], ring.sides[d],
            ))
        return copies

    def reduce(t, c, k):
        copies = []
        for d, way in ways:
            cols = columns(c, d, k == 0)
            copies.append(send(
                parts[t].at[ring.slot(way * (half - k)), :, cols],
                arriving.at[t, d, k, :, cols],
                reduce_send.at[t, c, d, k], reduce_recv.at[t, c, d, k], ring.sides[d],
            ))
        return copies

    def go(copies):
        for copy in copies:
            copy.start()

    def come(copies):
        for copy in copies:
            copy.wait_recv()

    def pass_on(t, c, k):
        def action():
            if k > 0:
                come(gather(t, c, k - 1))
            go(gather(t, c, k))
        return action

    def add_on(t, c, k):
        def action():
            if k > 0:
                come(reduce(t, c, k - 1))
                for d, way in ways:
                    slot, cols = ring.slot(way * (half - k)), columns(c, d, k == 1)
                    parts[t][slot, :, cols] = (
                        parts[t][slot, :, cols].astype(F32)
                        + arriving[t, d, k - 1, :, cols].astype(F32)
                    ).astype(BF16)
            go(reduce(t, c, k))
        return action

    def total_of(t, rows):
        return (
            parts[t][0, rows, :].astype(F32)
            + arriving[t, 0, half - 1, rows, :].astype(F32)
            + arriving[t, 1, half - 1, rows, :].astype(F32)
        )

    def weights_of(base):
        rows = flat(gates_ref).astype(F32)
        lane = lax.broadcasted_iota(jnp.int32, rows.shape, 1)
        for j in range(local):
            index = base + ring.me * local + j
            column = jnp.sum(jnp.where(lane == index, rows, 0.0), axis=1, keepdims=True)
            weight_ref[base // experts, j] = jnp.broadcast_to(column, rows.shape)

    tile, wide = tile_of(units), tile_of(width)
    inner = units // tile

    def weight_of(m, j):
        return jnp.concatenate([weight_ref[m, j]] * (tile // LANES), axis=1)

    def pre_activation(n):
        j, cols = n // inner, span(n % inner, tile)
        rows = flat(prev_ref)
        pre_gate[j, :, cols] = dot(rows, wg[j, :, cols], 1, 0)
        pre_up[j, :, cols] = dot(rows, wu[j, :, cols], 1, 0)

    def gradient(n):
        j, cols = n // inner, span(n % inner, tile)
        weight = weight_of(1, j)
        plain = dot(flat(cots_ref), wd[j, cols, :], 1, 1)
        gate, up = pre_gate[j, :, cols], pre_up[j, :, cols]
        sigma = jax.nn.sigmoid(gate)
        active = gate * sigma
        hidden = active * up
        d_hidden = weight * plain
        product = hidden * plain
        for i in range(tile // LANES):
            sums[j] += product[:, i * LANES : (i + 1) * LANES]
        gated[j, :, cols] = (weight * hidden).astype(BF16)
        d_gate[j, :, cols] = (d_hidden * up * sigma * (1.0 + gate * (1.0 - sigma))).astype(BF16)
        d_up[j, :, cols] = (d_hidden * active).astype(BF16)

    def row_gradient(first):
        def body(n):
            cols = span(first + n, wide)
            total = 0.0
            for j in range(local):
                total = total + dot(d_gate[j], wg[j, cols, :], 1, 1)
                total = total + dot(d_up[j], wu[j, cols, :], 1, 1)
            row_ref[:, :, cols] = total.astype(BF16).reshape(owners, tokens, wide)
        return body

    def hidden(n):
        j, cols = n // inner, span(n % inner, tile)
        rows = flat(next_ref)
        gate = dot(rows, wg[j, :, cols], 1, 0)
        up = dot(rows, wu[j, :, cols], 1, 0)
        hidden_ref[j, :, cols] = (
            weight_of(0, j) * (gate * jax.nn.sigmoid(gate) * up)
        ).astype(BF16)

    def mix(first):
        def body(n):
            cols = span(first + n, wide)
            total = 0.0
            for j in range(local):
                total = total + dot(hidden_ref[j], wd[j, :, cols], 1, 0)
            part_ref[:, :, cols] = total.astype(BF16).reshape(owners, tokens, wide)
        return body

    steps, deep = width // wide, units // tile

    def outer_gradient(n):
        j, rows = n // steps, span(n % steps, wide)
        left = prev_ref[:, :, rows].reshape(-1, wide)
        wg[j, rows, :] = dot(left, d_gate[j], 0, 0).astype(BF16)
        wu[j, rows, :] = dot(left, d_up[j], 0, 0).astype(BF16)

    def down_gradient(n):
        j, rows = n // deep, span(n % deep, tile)
        wd[j, rows, :] = dot(gated[j, :, rows], flat(cots_ref), 0, 0).astype(BF16)

    def small(source, target, sends, receives, own):
        return [
            send(
                source.at[0 if own else ring.slot(r)], target.at[ring.slot(-r)],
                sends.at[r - 1], receives.at[r - 1], ring.device(r),
            )
            for r in range(1, owners)
        ]

    def return_products():
        lane = lax.broadcasted_iota(jnp.int32, sums.shape[1:], 1)
        total = jnp.zeros(sums.shape[1:], F32)
        for j in range(local):
            column = jnp.sum(sums[j], axis=1, keepdims=True)
            total = jnp.where(lane == ring.me * local + j, column, total)
        products_ref[...] = total.astype(BF16).reshape(products_ref.shape)
        go(small(products_ref, returned_ref, product_send, product_recv, False))
        returned_ref[0] = products_ref[0]

    def backward():
        come(small(products_ref, returned_ref, product_send, product_recv, False))
        by_expert = jnp.sum(returned_ref[...].astype(F32), axis=0).astype(BF16)
        turned = dot(eye(LANES), by_expert, 1, 1)
        name = lax.broadcasted_iota(jnp.int32, turned.shape, 0)
        names = routes_prev_ref[...]
        picks = [
            jnp.sum(jnp.where(names[k : k + 1] == name, turned, 0.0), axis=0, keepdims=True)
            for k in range(names.shape[0])
        ]
        gate_grad_ref[...] = jnp.concatenate(picks, axis=0).astype(BF16)
        for c in range(CHUNKS):
            come(reduce(ROW, c, half - 1))

        @pl.loop(0, tokens // GROUP)
        def _(i):
            rows = span(i, GROUP)
            values = stash_ref[rows, :].astype(F32)
            scale = scale_of(values)
            unit = values * scale
            change = total_of(ROW, rows) * gain_ref[...].astype(F32)
            mean = jnp.mean(change * unit, axis=-1, keepdims=True)
            bwd_ref[rows, :] = (
                cots_ref[0, rows, :].astype(F32) + scale * (change - unit * mean)
            ).astype(BF16)

    def forward():
        for c in range(CHUNKS):
            come(reduce(MIX, c, half - 1))

        @pl.loop(0, tokens // GROUP)
        def _(i):
            rows = span(i, GROUP)
            fwd_ref[rows, :] = (arrived_ref[rows, :].astype(F32) + total_of(MIX, rows)).astype(BF16)

    cot_shift = send(cot_ref, cots_ref.at[0], shift_send.at[0], shift_recv.at[0], ring.shifted(-1))
    act_shift = send(act_ref, arrived_ref, shift_send.at[1], shift_recv.at[1], ring.shifted(1))
    both = range(CHUNKS)

    normalize(stash_ref, prev_ref)
    dense_gates()
    met()
    cot_shift.start()
    for c in both:
        pass_on(PREV, c, 0)()
    gate_copies = small(gates_ref, gates_ref, gate_send, gate_recv, True)
    go(gate_copies)
    sums[...] = jnp.zeros(sums.shape, F32)
    cot_shift.wait()
    act_shift.start()
    for c in both:
        pass_on(COT, c, 0)()
    for k in range(1, half):
        for c in both:
            pass_on(PREV, c, k)()
        if k == 1:
            act_shift.wait()
            normalize(arrived_ref, next_ref)
    cots = [pass_on(COT, c, k) for k in range(1, half) for c in both]
    nexts = [pass_on(NEXT, c, k) for k in range(half) for c in both]
    for action in cots[:CHUNKS] + nexts[:1]:
        action()
    come(gate_copies)
    for base in (0, experts):
        weights_of(base)
    for copy in loads:
        copy.wait()
    for c in both:
        come(gather(PREV, c, half - 1))
    run(local * inner, pre_activation, cots[CHUNKS:-CHUNKS])
    for action in (cots[-2], nexts[1], cots[-1], nexts[2]):
        action()
    for c in both:
        come(gather(COT, c, half - 1))
    split = steps // CHUNKS
    run(local * inner, gradient, nexts[3:-2])
    run(split, row_gradient(0), nexts[-2:-1])
    add_on(ROW, 0, 0)()
    nexts[-1]()
    for c in range(1, CHUNKS):
        run(split, row_gradient(c * split))
        add_on(ROW, c, 0)()
    return_products()
    for c in both:
        come(gather(NEXT, c, half - 1))
    rows = [add_on(ROW, c, k) for k in range(1, half) for c in both]
    mixes = [add_on(MIX, c, k) for k in range(1, half) for c in both]
    run(local * inner, hidden, rows[:-CHUNKS])
    for c in both:
        run(split, mix(c * split), rows[c - CHUNKS : len(rows) + c - CHUNKS + 1])
        add_on(MIX, c, 0)()
    backward()
    run(local * steps, outer_gradient, mixes[:-CHUNKS])
    run(local * deep, down_gradient, mixes[-CHUNKS:])
    forward()
    for c in both:
        for k in range(half):
            for copies in [gather(t, c, k) for t in range(3)] + [reduce(t, c, k) for t in range(2)]:
                for copy in copies:
                    copy.wait_send()
    act_products = small(products_ref, returned_ref, product_send, product_recv, False)
    for copy in gate_copies + act_products:
        copy.wait_send()


def tick_call(sections, owners, act, stash, cot, gain, choices, weights):
    tokens, width = stash.shape
    local, _, units = weights[0].shape
    half = owners // 2
    every = pltpu.VMEM((owners, tokens, width), BF16)
    inner = (local, owners * tokens, units)
    lanes = (local, owners * tokens, LANES)
    small = pltpu.VMEM((owners, tokens, LANES), BF16)
    peers = pltpu.SemaphoreType.DMA((owners - 1,))
    held = sum(w.size for w in weights) * jnp.dtype(BF16).itemsize
    return pl.pallas_call(
        functools.partial(tick_kernel, sections, owners),
        out_shape=(
            pltpu.VMEM((tokens, width), BF16),
            pltpu.VMEM((tokens, width), BF16),
            pltpu.VMEM(choices[0].shape, BF16),
        )
        + tuple(pltpu.VMEM(w.shape, BF16) for w in weights),
        in_specs=[VMEM] * 8 + [ANY] * 3,
        out_specs=(VMEM,) * 6,
        scratch_shapes=[pltpu.VMEM((tokens, width), BF16)]
        + [every] * 5
        + [pltpu.VMEM((2, 2, half, tokens, width), BF16)]
        + [small] * 3
        + [pltpu.VMEM((2,) + lanes, F32), pltpu.VMEM(lanes, F32)]
        + [pltpu.VMEM(inner, F32)] * 2
        + [pltpu.VMEM(inner, BF16)] * 4
        + [pltpu.SemaphoreType.DMA((2,))] * 2
        + [peers] * 4
        + [pltpu.SemaphoreType.DMA((3, CHUNKS, 2, half))] * 2
        + [pltpu.SemaphoreType.DMA((2, CHUNKS, 2, half))] * 2
        + [pltpu.SemaphoreType.DMA((3,))],
        compiler_params=pltpu.CompilerParams(
            collective_id=0, has_side_effects=True, vmem_limit_bytes=VMEM_LIMIT - held
        ),
    )(act, stash, cot, gain, *choices, *weights)


def per_device(
    sent_acts,
    stash,
    cotangents,
    norm_gain,
    w_gate,
    w_up,
    w_down,
    routes_next,
    gates_next,
    routes_prev,
    gates_prev,
):
    choices = [jnp.swapaxes(a[0], 0, 1) for a in (routes_next, gates_next, routes_prev, gates_prev)]
    fwd, bwd, gate_grad, *grads = tick_call(
        lax.axis_size("section"), lax.axis_size("expert"),
        sent_acts[0], stash[0], cotangents[0], norm_gain, choices, (w_gate[0], w_up[0], w_down[0]),
    )
    return (fwd[None], bwd[None], jnp.swapaxes(gate_grad, 0, 1)[None]) + tuple(g[None] for g in grads)


def solution(mesh):
    tokens = P("section", "expert", None)
    weights = P("section", "expert", None, None)
    return jax.shard_map(
        per_device,
        mesh=mesh,
        in_specs=(tokens, tokens, tokens, P("section", None), weights, weights, weights)
        + (tokens,) * 4,
        out_specs=(tokens, tokens, tokens, weights, weights, weights),
        check_vma=False,
    )
```

```python
import functools

import jax
import jax.numpy as jnp
from jax import lax
from jax.experimental import pallas as pl
from jax.experimental.pallas import tpu as pltpu
from jax.sharding import PartitionSpec as P

EPS = 1e-06
F32 = jnp.float32
BF16 = jnp.bfloat16
LANES = 128
GROUP = 16
CHUNKS = 2
PREV, COT, NEXT = 0, 1, 2
ROW, MIX = 0, 1
VMEM = pl.BlockSpec(memory_space=pltpu.VMEM)
ANY = pl.BlockSpec(memory_space=pl.ANY)
VMEM_LIMIT = 61 * 2**20
STORE_LIMIT = 4 * 2**20


class Ring:
    def __init__(self, sections, owners):
        bits = owners.bit_length() - 1
        self.n = owners
        self.half = owners // 2
        self.nz = 1 << ((bits + 1) // 2)
        self.ny = owners // self.nz
        self.section = lax.axis_index("section")
        self.sections = sections
        self.me = lax.axis_index("expert")
        z, y = self.me // self.ny, self.me % self.ny
        self.place = y * self.nz + z + (y % 2) * (self.nz - 1 - 2 * z)
        self.sides = (self.device(1), self.device(-1))

    def device(self, offset):
        p = (self.place + offset + self.n) % self.n
        y, r = p // self.nz, p % self.nz
        return (self.section, (r + (y % 2) * (self.nz - 1 - 2 * r)) * self.ny + y)

    def shifted(self, by):
        return ((self.section + by + self.sections) % self.sections, self.me)

    def slot(self, offset):
        offset = (offset + self.n) % self.n
        if offset > self.half:
            return 2 * (self.n - offset) - 1
        return 2 * offset - (offset == self.half)

    def greet(self):
        barrier = pltpu.get_barrier_semaphore()
        targets = [self.device(r) for r in range(1, self.n)]
        targets += [self.shifted(1), self.shifted(-1)]
        for target in targets:
            pl.semaphore_signal(
                barrier, inc=1, device_id=target, device_id_type=pl.DeviceIdType.MESH
            )
        return lambda: pl.semaphore_wait(barrier, len(targets))


def send(src, dst, send_sem, recv_sem, device):
    return pltpu.make_async_remote_copy(
        src_ref=src,
        dst_ref=dst,
        send_sem=send_sem,
        recv_sem=recv_sem,
        device_id=device,
        device_id_type=pl.DeviceIdType.MESH,
    )


def scale_of(values):
    return lax.rsqrt(jnp.mean(values * values, axis=-1, keepdims=True) + EPS)


def dot(a, b, ca, cb):
    return lax.dot_general(a, b, (((ca,), (cb,)), ((), ())), preferred_element_type=F32)


def flat(ref):
    value = ref[...]
    return value.reshape(-1, value.shape[-1])


def tile_of(size):
    return 256 if size % 256 == 0 else LANES


def span(i, size):
    return pl.ds(pl.multiple_of(i * size, size), size)


def eye(size):
    shape = (size, size)
    row, col = (lax.broadcasted_iota(jnp.int32, shape, d) for d in range(2))
    return (row == col).astype(BF16)


def run(count, body, actions=()):
    table = {}
    for n, action in enumerate(actions):
        table.setdefault((2 * n + 1) * count // (2 * len(actions)), []).append(action)

    @pl.loop(0, count)
    def _(i):
        for at, group in table.items():
            @pl.when(i == at)
            def _():
                for action in group:
                    action()
        body(i)


def tick_kernel(
    sections, owners,
    act_ref, stash_ref, cot_ref, gain_ref,
    routes_next_ref, choice_next_ref, routes_prev_ref, choice_prev_ref,
    wg_hbm, wu_hbm, wd_hbm,
    fwd_ref, bwd_ref, gate_grad_ref, wg, wu, wd,
    arrived_ref, prev_ref, cots_ref, next_ref, row_ref, part_ref, arriving,
    gates_ref, products_ref, returned_ref, weight_ref, sums,
    pre_gate, pre_up, d_gate, d_up, gated, hidden_ref,
    shift_send, shift_recv, gate_send, gate_recv, product_send, product_recv,
    gather_send, gather_recv, reduce_send, reduce_recv, weight_sem,
):
    ring = Ring(sections, owners)
    half = ring.half
    tokens, width = stash_ref.shape
    local, _, units = wg.shape
    experts = local * owners
    chunk = width // CHUNKS
    loads = [
        pltpu.make_async_copy(h, v, weight_sem.at[i])
        for i, (h, v) in enumerate(((wg_hbm, wg), (wu_hbm, wu), (wd_hbm, wd)))
    ]
    for copy in loads:
        copy.start()
    met = ring.greet()

    def normalize(source, target):
        @pl.loop(0, tokens // GROUP)
        def _(i):
            rows = span(i, GROUP)
            values = source[rows, :].astype(F32)
            target[0, rows, :] = (values * scale_of(values) * gain_ref[...].astype(F32)).astype(BF16)

    def dense_gates():
        lane = lax.broadcasted_iota(jnp.int32, (LANES, tokens), 0)
        total = jnp.zeros((LANES, tokens), F32)
        for base, routes, gates in (
            (0, routes_next_ref, choice_next_ref), (experts, routes_prev_ref, choice_prev_ref)
        ):
            names, values = routes[...] + base, gates[...].astype(F32)
            for k in range(names.shape[0]):
                total += jnp.where(names[k : k + 1] == lane, values[k : k + 1], 0.0)
        gates_ref[0] = dot(eye(tokens), total.astype(BF16), 1, 1).astype(BF16)

    buffers, parts = (prev_ref, cots_ref, next_ref), (row_ref, part_ref)
    ways = ((0, 1), (1, -1))

    def columns(c, d, cut):
        return pl.ds(c * chunk + d * (chunk // 2), chunk // 2) if cut else pl.ds(c * chunk, chunk)

    def gather(t, c, k):
        copies = []
        for d, way in ways:
            cols = columns(c, d, k == half - 1)
            copies.append(send(
                buffers[t].at[ring.slot(-way * k), :, cols],
                buffers[t].at[ring.slot(-way * (k + 1)), :, cols],
                gather_send.at[t, c, d, k], gather_recv.at[t, c, d, k], ring.sides[d],
            ))
        return copies

    def reduce(t, c, k):
        copies = []
        for d, way in ways:
            cols = columns(c, d, k == 0)
            copies.append(send(
                parts[t].at[ring.slot(way * (half - k)), :, cols],
                arriving.at[t, d, k, :, cols],
                reduce_send.at[t, c, d, k], reduce_recv.at[t, c, d, k], ring.sides[d],
            ))
        return copies

    def go(copies):
        for copy in copies:
            copy.start()

    def come(copies):
        for copy in copies:
            copy.wait_recv()

    def pass_on(t, c, k):
        def action():
            if k > 0:
                come(gather(t, c, k - 1))
            go(gather(t, c, k))
        return action

    def add_on(t, c, k):
        def action():
            if k > 0:
                come(reduce(t, c, k - 1))
                for d, way in ways:
                    slot, cols = ring.slot(way * (half - k)), columns(c, d, k == 1)
                    parts[t][slot, :, cols] = (
                        parts[t][slot, :, cols].astype(F32)
                        + arriving[t, d, k - 1, :, cols].astype(F32)
                    ).astype(BF16)
            go(reduce(t, c, k))
        return action

    def total_of(t, rows):
        return (
            parts[t][0, rows, :].astype(F32)
            + arriving[t, 0, half - 1, rows, :].astype(F32)
            + arriving[t, 1, half - 1, rows, :].astype(F32)
        )

    def weights_of(base):
        rows = flat(gates_ref).astype(F32)
        lane = lax.broadcasted_iota(jnp.int32, rows.shape, 1)
        for j in range(local):
            index = base + ring.me * local + j
            column = jnp.sum(jnp.where(lane == index, rows, 0.0), axis=1, keepdims=True)
            weight_ref[base // experts, j] = jnp.broadcast_to(column, rows.shape)

    tile, wide = tile_of(units), tile_of(width)
    inner = units // tile

    def weight_of(m, j):
        return jnp.concatenate([weight_ref[m, j]] * (tile // LANES), axis=1)

    def pre_activation(n):
        j, cols = n // inner, span(n % inner, tile)
        rows = flat(prev_ref)
        pre_gate[j, :, cols] = dot(rows, wg[j, :, cols], 1, 0)
        pre_up[j, :, cols] = dot(rows, wu[j, :, cols], 1, 0)

    def gradient(n):
        j, cols = n // inner, span(n % inner, tile)
        weight = weight_of(1, j)
        plain = dot(flat(cots_ref), wd[j, cols, :], 1, 1)
        gate, up = pre_gate[j, :, cols], pre_up[j, :, cols]
        sigma = jax.nn.sigmoid(gate)
        active = gate * sigma
        hidden = active * up
        d_hidden = weight * plain
        product = hidden * plain
        for i in range(tile // LANES):
            sums[j] += product[:, i * LANES : (i + 1) * LANES]
        gated[j, :, cols] = (weight * hidden).astype(BF16)
        d_gate[j, :, cols] = (d_hidden * up * sigma * (1.0 + gate * (1.0 - sigma))).astype(BF16)
        d_up[j, :, cols] = (d_hidden * active).astype(BF16)

    def row_gradient(first):
        def body(n):
            cols = span(first + n, wide)
            total = 0.0
            for j in range(local):
                total = total + dot(d_gate[j], wg[j, cols, :], 1, 1)
                total = total + dot(d_up[j], wu[j, cols, :], 1, 1)
            row_ref[:, :, cols] = total.astype(BF16).reshape(owners, tokens, wide)
        return body

    def hidden(n):
        j, cols = n // inner, span(n % inner, tile)
        rows = flat(next_ref)
        gate = dot(rows, wg[j, :, cols], 1, 0)
        up = dot(rows, wu[j, :, cols], 1, 0)
        hidden_ref[j, :, cols] = (
            weight_of(0, j) * (gate * jax.nn.sigmoid(gate) * up)
        ).astype(BF16)

    def mix(first):
        def body(n):
            cols = span(first + n, wide)
            total = 0.0
            for j in range(local):
                total = total + dot(hidden_ref[j], wd[j, :, cols], 1, 0)
            part_ref[:, :, cols] = total.astype(BF16).reshape(owners, tokens, wide)
        return body

    steps, deep = width // wide, units // tile

    def outer_gradient(n):
        j, rows = n // steps, span(n % steps, wide)
        left = prev_ref[:, :, rows].reshape(-1, wide)
        wg[j, rows, :] = dot(left, d_gate[j], 0, 0).astype(BF16)
        wu[j, rows, :] = dot(left, d_up[j], 0, 0).astype(BF16)

    def down_gradient(n):
        j, rows = n // deep, span(n % deep, tile)
        wd[j, rows, :] = dot(gated[j, :, rows], flat(cots_ref), 0, 0).astype(BF16)

    def small(source, target, sends, receives, own):
        return [
            send(
                source.at[0 if own else ring.slot(r)], target.at[ring.slot(-r)],
                sends.at[r - 1], receives.at[r - 1], ring.device(r),
            )
            for r in range(1, owners)
        ]

    def return_products():
        lane = lax.broadcasted_iota(jnp.int32, sums.shape[1:], 1)
        total = jnp.zeros(sums.shape[1:], F32)
        for j in range(local):
            column = jnp.sum(sums[j], axis=1, keepdims=True)
            total = jnp.where(lane == ring.me * local + j, column, total)
        products_ref[...] = total.astype(BF16).reshape(products_ref.shape)
        go(small(products_ref, returned_ref, product_send, product_recv, False))
        returned_ref[0] = products_ref[0]

    def backward():
        come(small(products_ref, returned_ref, product_send, product_recv, False))
        by_expert = jnp.sum(returned_ref[...].astype(F32), axis=0).astype(BF16)
        turned = dot(eye(LANES), by_expert, 1, 1)
        name = lax.broadcasted_iota(jnp.int32, turned.shape, 0)
        names = routes_prev_ref[...]
        picks = [
            jnp.sum(jnp.where(names[k : k + 1] == name, turned, 0.0), axis=0, keepdims=True)
            for k in range(names.shape[0])
        ]
        gate_grad_ref[...] = jnp.concatenate(picks, axis=0).astype(BF16)
        for c in range(CHUNKS):
            come(reduce(ROW, c, half - 1))

        @pl.loop(0, tokens // GROUP)
        def _(i):
            rows = span(i, GROUP)
            values = stash_ref[rows, :].astype(F32)
            scale = scale_of(values)
            unit = values * scale
            change = total_of(ROW, rows) * gain_ref[...].astype(F32)
            mean = jnp.mean(change * unit, axis=-1, keepdims=True)
            bwd_ref[rows, :] = (
                cots_ref[0, rows, :].astype(F32) + scale * (change - unit * mean)
            ).astype(BF16)

    def forward():
        for c in range(CHUNKS):
            come(reduce(MIX, c, half - 1))

        @pl.loop(0, tokens // GROUP)
        def _(i):
            rows = span(i, GROUP)
            fwd_ref[rows, :] = (arrived_ref[rows, :].astype(F32) + total_of(MIX, rows)).astype(BF16)

    cot_shift = send(cot_ref, cots_ref.at[0], shift_send.at[0], shift_recv.at[0], ring.shifted(-1))
    act_shift = send(act_ref, arrived_ref, shift_send.at[1], shift_recv.at[1], ring.shifted(1))
    both = range(CHUNKS)

    normalize(stash_ref, prev_ref)
    dense_gates()
    met()
    cot_shift.start()
    for c in both:
        pass_on(PREV, c, 0)()
    gate_copies = small(gates_ref, gates_ref, gate_send, gate_recv, True)
    go(gate_copies)
    sums[...] = jnp.zeros(sums.shape, F32)
    cot_shift.wait()
    act_shift.start()
    for c in both:
        pass_on(COT, c, 0)()
    for k in range(1, half):
        for c in both:
            pass_on(PREV, c, k)()
        if k == 1:
            act_shift.wait()
            normalize(arrived_ref, next_ref)
    cots = [pass_on(COT, c, k) for k in range(1, half) for c in both]
    nexts = [pass_on(NEXT, c, k) for k in range(half) for c in both]
    for action in cots[:CHUNKS] + nexts[:1]:
        action()
    come(gate_copies)
    for base in (0, experts):
        weights_of(base)
    for copy in loads:
        copy.wait()
    for c in both:
        come(gather(PREV, c, half - 1))
    run(local * inner, pre_activation, cots[CHUNKS:-CHUNKS])
    for action in (cots[-2], nexts[1], cots[-1], nexts[2]):
        action()
    for c in both:
        come(gather(COT, c, half - 1))
    split = steps // CHUNKS
    run(local * inner, gradient, nexts[3:-2])
    run(split, row_gradient(0), nexts[-2:-1])
    add_on(ROW, 0, 0)()
    nexts[-1]()
    for c in range(1, CHUNKS):
        run(split, row_gradient(c * split))
        add_on(ROW, c, 0)()
    return_products()
    for c in both:
        come(gather(NEXT, c, half - 1))
    rows = [add_on(ROW, c, k) for k in range(1, half) for c in both]
    mixes = [add_on(MIX, c, k) for k in range(1, half) for c in both]
    run(local * inner, hidden, rows[:-CHUNKS])
    for c in both:
        run(split, mix(c * split), rows[c - CHUNKS : len(rows) + c - CHUNKS + 1])
        add_on(MIX, c, 0)()
    backward()
    run(local * steps, outer_gradient, mixes[:-CHUNKS])
    run(local * deep, down_gradient, mixes[-CHUNKS:])
    forward()
    for c in both:
        for k in range(half):
            for copies in [gather(t, c, k) for t in range(3)] + [reduce(t, c, k) for t in range(2)]:
                for copy in copies:
                    copy.wait_send()
    act_products = small(products_ref, returned_ref, product_send, product_recv, False)
    for copy in gate_copies + act_products:
        copy.wait_send()


def tick_call(sections, owners, act, stash, cot, gain, choices, weights):
    tokens, width = stash.shape
    local, _, units = weights[0].shape
    half = owners // 2
    every = pltpu.VMEM((owners, tokens, width), BF16)
    inner = (local, owners * tokens, units)
    lanes = (local, owners * tokens, LANES)
    small = pltpu.VMEM((owners, tokens, LANES), BF16)
    peers = pltpu.SemaphoreType.DMA((owners - 1,))
    held = sum(w.size for w in weights) * jnp.dtype(BF16).itemsize
    return pl.pallas_call(
        functools.partial(tick_kernel, sections, owners),
        out_shape=(
            pltpu.VMEM((tokens, width), BF16),
            pltpu.VMEM((tokens, width), BF16),
            pltpu.VMEM(choices[0].shape, BF16),
        )
        + tuple(pltpu.VMEM(w.shape, BF16) for w in weights),
        in_specs=[VMEM] * 8 + [ANY] * 3,
        out_specs=(VMEM,) * 6,
        scratch_shapes=[pltpu.VMEM((tokens, width), BF16)]
        + [every] * 5
        + [pltpu.VMEM((2, 2, half, tokens, width), BF16)]
        + [small] * 3
        + [pltpu.VMEM((2,) + lanes, F32), pltpu.VMEM(lanes, F32)]
        + [pltpu.VMEM(inner, F32)] * 2
        + [pltpu.VMEM(inner, BF16)] * 4
        + [pltpu.SemaphoreType.DMA((2,))] * 2
        + [peers] * 4
        + [pltpu.SemaphoreType.DMA((3, CHUNKS, 2, half))] * 2
        + [pltpu.SemaphoreType.DMA((2, CHUNKS, 2, half))] * 2
        + [pltpu.SemaphoreType.DMA((3,))],
        compiler_params=pltpu.CompilerParams(
            collective_id=0, has_side_effects=True, vmem_limit_bytes=VMEM_LIMIT - held
        ),
    )(act, stash, cot, gain, *choices, *weights)


def store_kernel(count, *refs):
    sem = refs[2 * count]
    copies = [
        pltpu.make_async_copy(v.at[i], h.at[i], sem.at[n, i])
        for n, (v, h) in enumerate(zip(refs[:count], refs[count : 2 * count]))
        for i in range(v.shape[0])
    ]
    for copy in copies:
        copy.start()
    for copy in copies:
        copy.wait()


def store(arrays):
    count, most = len(arrays), max(a.shape[0] for a in arrays)
    return pl.pallas_call(
        functools.partial(store_kernel, count),
        out_shape=tuple(jax.ShapeDtypeStruct(a.shape, a.dtype) for a in arrays),
        in_specs=[ANY] * count,
        out_specs=(ANY,) * count,
        scratch_shapes=[pltpu.SemaphoreType.DMA((count, most))],
        compiler_params=pltpu.CompilerParams(vmem_limit_bytes=STORE_LIMIT),
    )(*(pltpu.with_memory_space_constraint(a, pltpu.VMEM) for a in arrays))


def per_device(
    sent_acts,
    stash,
    cotangents,
    norm_gain,
    w_gate,
    w_up,
    w_down,
    routes_next,
    gates_next,
    routes_prev,
    gates_prev,
):
    choices = [jnp.swapaxes(a[0], 0, 1) for a in (routes_next, gates_next, routes_prev, gates_prev)]
    fwd, bwd, gate_grad, *grads = tick_call(
        lax.axis_size("section"), lax.axis_size("expert"),
        sent_acts[0], stash[0], cotangents[0], norm_gain, choices, (w_gate[0], w_up[0], w_down[0]),
    )
    fwd, bwd, gate_grad, *grads = store((fwd[None], bwd[None], gate_grad[None], *grads))
    return (fwd, bwd, jnp.swapaxes(gate_grad, 1, 2)) + tuple(g[None] for g in grads)


def solution(mesh):
    tokens = P("section", "expert", None)
    weights = P("section", "expert", None, None)
    return jax.shard_map(
        per_device,
        mesh=mesh,
        in_specs=(tokens, tokens, tokens, P("section", None), weights, weights, weights)
        + (tokens,) * 4,
        out_specs=(tokens, tokens, tokens, weights, weights, weights),
        check_vma=False,
    )
```

```python
import functools

import jax
import jax.numpy as jnp
from jax import lax
from jax.experimental import pallas as pl
from jax.experimental.pallas import tpu as pltpu
from jax.sharding import PartitionSpec as P

EPS = 1e-06
F32 = jnp.float32
BF16 = jnp.bfloat16
LANES = 128
GROUP = 16
CHUNKS = 2
PREV, COT, NEXT = 0, 1, 2
ROW, MIX = 0, 1
VMEM = pl.BlockSpec(memory_space=pltpu.VMEM)
ANY = pl.BlockSpec(memory_space=pl.ANY)
VMEM_LIMIT = 61 * 2**20
STORE_LIMIT = 4 * 2**20


class Ring:
    def __init__(self, sections, owners):
        bits = owners.bit_length() - 1
        self.n = owners
        self.half = owners // 2
        self.nz = 1 << ((bits + 1) // 2)
        self.ny = owners // self.nz
        self.section = lax.axis_index("section")
        self.sections = sections
        self.me = lax.axis_index("expert")
        z, y = self.me // self.ny, self.me % self.ny
        self.place = y * self.nz + z + (y % 2) * (self.nz - 1 - 2 * z)
        self.sides = (self.device(1), self.device(-1))

    def device(self, offset):
        p = (self.place + offset + self.n) % self.n
        y, r = p // self.nz, p % self.nz
        return (self.section, (r + (y % 2) * (self.nz - 1 - 2 * r)) * self.ny + y)

    def shifted(self, by):
        return ((self.section + by + self.sections) % self.sections, self.me)

    def slot(self, offset):
        offset = (offset + self.n) % self.n
        if offset > self.half:
            return 2 * (self.n - offset) - 1
        return 2 * offset - (offset == self.half)

    def greet(self):
        barrier = pltpu.get_barrier_semaphore()
        targets = [self.device(r) for r in range(1, self.n)]
        targets += [self.shifted(1), self.shifted(-1)]
        for target in targets:
            pl.semaphore_signal(
                barrier, inc=1, device_id=target, device_id_type=pl.DeviceIdType.MESH
            )
        return lambda: pl.semaphore_wait(barrier, len(targets))


def send(src, dst, send_sem, recv_sem, device):
    return pltpu.make_async_remote_copy(
        src_ref=src,
        dst_ref=dst,
        send_sem=send_sem,
        recv_sem=recv_sem,
        device_id=device,
        device_id_type=pl.DeviceIdType.MESH,
    )


def scale_of(values):
    return lax.rsqrt(jnp.mean(values * values, axis=-1, keepdims=True) + EPS)


def dot(a, b, ca, cb):
    return lax.dot_general(a, b, (((ca,), (cb,)), ((), ())), preferred_element_type=F32)


def flat(ref):
    value = ref[...]
    return value.reshape(-1, value.shape[-1])


def tile_of(size):
    return 256 if size % 256 == 0 else LANES


def span(i, size):
    return pl.ds(pl.multiple_of(i * size, size), size)


def eye(size):
    shape = (size, size)
    row, col = (lax.broadcasted_iota(jnp.int32, shape, d) for d in range(2))
    return (row == col).astype(BF16)


def run(count, body, actions=()):
    table = {}
    for n, action in enumerate(actions):
        table.setdefault((2 * n + 1) * count // (2 * len(actions)), []).append(action)

    @pl.loop(0, count)
    def _(i):
        for at, group in table.items():
            @pl.when(i == at)
            def _():
                for action in group:
                    action()
        body(i)


def tick_kernel(
    sections, owners,
    act_ref, stash_ref, cot_ref, gain_ref,
    routes_next_ref, choice_next_ref, routes_prev_ref, choice_prev_ref,
    wg_hbm, wu_hbm, wd_hbm,
    fwd_ref, bwd_ref, gate_grad_ref, wg, wu, wd,
    arrived_ref, prev_ref, cots_ref, next_ref, row_ref, part_ref, arriving,
    dense_ref, gates_ref, products_ref, returned_ref, weight_ref, sums,
    pre_gate, pre_up, d_gate, d_up, gated, hidden_ref,
    shift_send, shift_recv, gate_send, gate_recv, product_send, product_recv,
    gather_send, gather_recv, reduce_send, reduce_recv, weight_sem,
):
    ring = Ring(sections, owners)
    half = ring.half
    tokens, width = stash_ref.shape
    local, _, units = wg.shape
    chunk = width // CHUNKS
    loads = [
        pltpu.make_async_copy(h, v, weight_sem.at[i])
        for i, (h, v) in enumerate(((wg_hbm, wg), (wu_hbm, wu), (wd_hbm, wd)))
    ]
    for copy in loads:
        copy.start()
    met = ring.greet()

    def normalize(source, target):
        @pl.loop(0, tokens // GROUP)
        def _(i):
            rows = span(i, GROUP)
            values = source[rows, :].astype(F32)
            target[0, rows, :] = (values * scale_of(values) * gain_ref[...].astype(F32)).astype(BF16)

    def padded(rows):
        rest = jnp.zeros((dense_ref.shape[1] - len(rows), tokens), F32)
        return jnp.concatenate(rows + [rest], axis=0).astype(BF16)

    def dense_gates():
        for r in range(owners):
            first = ring.device(r)[1] * local
            rows = []
            for routes, gates in ((routes_next_ref, choice_next_ref), (routes_prev_ref, choice_prev_ref)):
                for j in range(local):
                    hit = jnp.where(routes[...] == first + j, gates[...].astype(F32), 0.0)
                    rows.append(jnp.sum(hit, axis=0, keepdims=True))
            dense_ref[ring.slot(r)] = padded(rows)
        gates_ref[0] = dense_ref[0]

    buffers, parts = (prev_ref, cots_ref, next_ref), (row_ref, part_ref)
    ways = ((0, 1), (1, -1))

    def columns(c, d, cut):
        return pl.ds(c * chunk + d * (chunk // 2), chunk // 2) if cut else pl.ds(c * chunk, chunk)

    def gather(t, c, k):
        copies = []
        for d, way in ways:
            cols = columns(c, d, k == half - 1)
            copies.append(send(
                buffers[t].at[ring.slot(-way * k), :, cols],
                buffers[t].at[ring.slot(-way * (k + 1)), :, cols],
                gather_send.at[t, c, d, k], gather_recv.at[t, c, d, k], ring.sides[d],
            ))
        return copies

    def reduce(t, c, k):
        copies = []
        for d, way in ways:
            cols = columns(c, d, k == 0)
            copies.append(send(
                parts[t].at[ring.slot(way * (half - k)), :, cols],
                arriving.at[t, d, k, :, cols],
                reduce_send.at[t, c, d, k], reduce_recv.at[t, c, d, k], ring.sides[d],
            ))
        return copies

    def go(copies):
        for copy in copies:
            copy.start()

    def come(copies):
        for copy in copies:
            copy.wait_recv()

    def pass_on(t, c, k):
        def action():
            if k > 0:
                come(gather(t, c, k - 1))
            go(gather(t, c, k))
        return action

    def add_on(t, c, k):
        def action():
            if k > 0:
                come(reduce(t, c, k - 1))
                for d, way in ways:
                    slot, cols = ring.slot(way * (half - k)), columns(c, d, k == 1)
                    parts[t][slot, :, cols] = (
                        parts[t][slot, :, cols].astype(F32)
                        + arriving[t, d, k - 1, :, cols].astype(F32)
                    ).astype(BF16)
            go(reduce(t, c, k))
        return action

    def total_of(t, rows):
        return (
            parts[t][0, rows, :].astype(F32)
            + arriving[t, 0, half - 1, rows, :].astype(F32)
            + arriving[t, 1, half - 1, rows, :].astype(F32)
        )

    def spread_weights():
        diagonal, ones = eye(tokens), jnp.ones((tokens, LANES), BF16)

        @pl.loop(0, owners)
        def _(b):
            held = gates_ref[b]
            for m in range(2):
                for j in range(local):
                    row = held[m * local + j : m * local + j + 1]
                    weight_ref[m, j, span(b, tokens), :] = dot(diagonal * row, ones, 1, 0)

    tile, wide = tile_of(units), tile_of(width)
    inner = units // tile

    def weight_of(m, j):
        return jnp.concatenate([weight_ref[m, j]] * (tile // LANES), axis=1)

    def pre_activation(n):
        j, cols = n // inner, span(n % inner, tile)
        rows = flat(prev_ref)
        pre_gate[j, :, cols] = dot(rows, wg[j, :, cols], 1, 0)
        pre_up[j, :, cols] = dot(rows, wu[j, :, cols], 1, 0)

    def gradient(n):
        j, cols = n // inner, span(n % inner, tile)
        weight = weight_of(1, j)
        plain = dot(flat(cots_ref), wd[j, cols, :], 1, 1)
        gate, up = pre_gate[j, :, cols], pre_up[j, :, cols]
        sigma = jax.nn.sigmoid(gate)
        active = gate * sigma
        hidden = active * up
        d_hidden = weight * plain
        product = hidden * plain
        for i in range(tile // LANES):
            sums[j] += product[:, i * LANES : (i + 1) * LANES]
        gated[j, :, cols] = (weight * hidden).astype(BF16)
        d_gate[j, :, cols] = (d_hidden * up * sigma * (1.0 + gate * (1.0 - sigma))).astype(BF16)
        d_up[j, :, cols] = (d_hidden * active).astype(BF16)

    def row_gradient(first):
        def body(n):
            cols = span(first + n, wide)
            total = 0.0
            for j in range(local):
                total = total + dot(d_gate[j], wg[j, cols, :], 1, 1)
                total = total + dot(d_up[j], wu[j, cols, :], 1, 1)
            row_ref[:, :, cols] = total.astype(BF16).reshape(owners, tokens, wide)
        return body

    def hidden(n):
        j, cols = n // inner, span(n % inner, tile)
        rows = flat(next_ref)
        gate = dot(rows, wg[j, :, cols], 1, 0)
        up = dot(rows, wu[j, :, cols], 1, 0)
        hidden_ref[j, :, cols] = (
            weight_of(0, j) * (gate * jax.nn.sigmoid(gate) * up)
        ).astype(BF16)

    def mix(first):
        def body(n):
            cols = span(first + n, wide)
            total = 0.0
            for j in range(local):
                total = total + dot(hidden_ref[j], wd[j, :, cols], 1, 0)
            part_ref[:, :, cols] = total.astype(BF16).reshape(owners, tokens, wide)
        return body

    steps, deep = width // wide, units // tile

    def outer_gradient(n):
        j, rows = n // steps, span(n % steps, wide)
        left = prev_ref[:, :, rows].reshape(-1, wide)
        wg[j, rows, :] = dot(left, d_gate[j], 0, 0).astype(BF16)
        wu[j, rows, :] = dot(left, d_up[j], 0, 0).astype(BF16)

    def down_gradient(n):
        j, rows = n // deep, span(n % deep, tile)
        wd[j, rows, :] = dot(gated[j, :, rows], flat(cots_ref), 0, 0).astype(BF16)

    def small(source, target, sends, receives):
        return [
            send(
                source.at[ring.slot(r)], target.at[ring.slot(-r)],
                sends.at[r - 1], receives.at[r - 1], ring.device(r),
            )
            for r in range(1, owners)
        ]

    def return_products():
        ones = jnp.ones((dense_ref.shape[1], LANES), F32)

        @pl.loop(0, owners)
        def _(b):
            products_ref[b] = padded([
                lax.dot_general(
                    ones, sums[j, span(b, tokens), :], (((1,), (1,)), ((), ())),
                    precision=lax.Precision.HIGHEST, preferred_element_type=F32,
                )[:1]
                for j in range(local)
            ])

        go(small(products_ref, returned_ref, product_send, product_recv))
        returned_ref[0] = products_ref[0]

    def backward():
        come(small(products_ref, returned_ref, product_send, product_recv))
        total = jnp.zeros(gate_grad_ref.shape, F32)
        for r in range(owners):
            first, block = ring.device(r)[1] * local, returned_ref[ring.slot(r)].astype(F32)
            for j in range(local):
                total += jnp.where(routes_prev_ref[...] == first + j, block[j : j + 1], 0.0)
        gate_grad_ref[...] = total.astype(BF16)
        for c in range(CHUNKS):
            come(reduce(ROW, c, half - 1))

        @pl.loop(0, tokens // GROUP)
        def _(i):
            rows = span(i, GROUP)
            values = stash_ref[rows, :].astype(F32)
            scale = scale_of(values)
            unit = values * scale
            change = total_of(ROW, rows) * gain_ref[...].astype(F32)
            mean = jnp.mean(change * unit, axis=-1, keepdims=True)
            bwd_ref[rows, :] = (
                cots_ref[0, rows, :].astype(F32) + scale * (change - unit * mean)
            ).astype(BF16)

    def forward():
        for c in range(CHUNKS):
            come(reduce(MIX, c, half - 1))

        @pl.loop(0, tokens // GROUP)
        def _(i):
            rows = span(i, GROUP)
            fwd_ref[rows, :] = (arrived_ref[rows, :].astype(F32) + total_of(MIX, rows)).astype(BF16)

    cot_shift = send(cot_ref, cots_ref.at[0], shift_send.at[0], shift_recv.at[0], ring.shifted(-1))
    act_shift = send(act_ref, arrived_ref, shift_send.at[1], shift_recv.at[1], ring.shifted(1))
    both = range(CHUNKS)

    normalize(stash_ref, prev_ref)
    met()
    cot_shift.start()
    for c in both:
        pass_on(PREV, c, 0)()
    dense_gates()
    gate_copies = small(dense_ref, gates_ref, gate_send, gate_recv)
    go(gate_copies)
    sums[...] = jnp.zeros(sums.shape, F32)
    cot_shift.wait()
    act_shift.start()
    for c in both:
        pass_on(COT, c, 0)()
    for k in range(1, half):
        for c in both:
            pass_on(PREV, c, k)()
        if k == 1:
            act_shift.wait()
            normalize(arrived_ref, next_ref)
    cots = [pass_on(COT, c, k) for k in range(1, half) for c in both]
    nexts = [pass_on(NEXT, c, k) for k in range(half) for c in both]
    for action in cots[:CHUNKS] + nexts[:1]:
        action()
    come(gate_copies)
    spread_weights()
    for copy in loads:
        copy.wait()
    for c in both:
        come(gather(PREV, c, half - 1))
    run(local * inner, pre_activation, cots[CHUNKS:-CHUNKS])
    for action in (cots[-2], nexts[1], cots[-1], nexts[2]):
        action()
    for c in both:
        come(gather(COT, c, half - 1))
    split = steps // CHUNKS
    run(local * inner, gradient, nexts[3:-2])
    run(split, row_gradient(0), nexts[-2:-1])
    add_on(ROW, 0, 0)()
    nexts[-1]()
    for c in range(1, CHUNKS):
        run(split, row_gradient(c * split))
        add_on(ROW, c, 0)()
    return_products()
    for c in both:
        come(gather(NEXT, c, half - 1))
    rows = [add_on(ROW, c, k) for k in range(1, half) for c in both]
    mixes = [add_on(MIX, c, k) for k in range(1, half) for c in both]
    run(local * inner, hidden, rows[:-CHUNKS])
    for c in both:
        run(split, mix(c * split), rows[c - CHUNKS : len(rows) + c - CHUNKS + 1])
        add_on(MIX, c, 0)()
    backward()
    run(local * steps, outer_gradient, mixes[:-CHUNKS])
    run(local * deep, down_gradient, mixes[-CHUNKS:])
    forward()
    for c in both:
        for k in range(half):
            for copies in [gather(t, c, k) for t in range(3)] + [reduce(t, c, k) for t in range(2)]:
                for copy in copies:
                    copy.wait_send()
    act_products = small(products_ref, returned_ref, product_send, product_recv)
    for copy in gate_copies + act_products:
        copy.wait_send()


def tick_call(sections, owners, act, stash, cot, gain, choices, weights):
    tokens, width = stash.shape
    local, _, units = weights[0].shape
    half = owners // 2
    every = pltpu.VMEM((owners, tokens, width), BF16)
    inner = (local, owners * tokens, units)
    lanes = (local, owners * tokens, LANES)
    small = pltpu.VMEM((owners, -(-2 * local // 8) * 8, tokens), BF16)
    peers = pltpu.SemaphoreType.DMA((owners - 1,))
    held = sum(w.size for w in weights) * jnp.dtype(BF16).itemsize
    return pl.pallas_call(
        functools.partial(tick_kernel, sections, owners),
        out_shape=(
            pltpu.VMEM((tokens, width), BF16),
            pltpu.VMEM((tokens, width), BF16),
            pltpu.VMEM(choices[0].shape, BF16),
        )
        + tuple(pltpu.VMEM(w.shape, BF16) for w in weights),
        in_specs=[VMEM] * 8 + [ANY] * 3,
        out_specs=(VMEM,) * 6,
        scratch_shapes=[pltpu.VMEM((tokens, width), BF16)]
        + [every] * 5
        + [pltpu.VMEM((2, 2, half, tokens, width), BF16)]
        + [small] * 4
        + [pltpu.VMEM((2,) + lanes, F32), pltpu.VMEM(lanes, F32)]
        + [pltpu.VMEM(inner, F32)] * 2
        + [pltpu.VMEM(inner, BF16)] * 4
        + [pltpu.SemaphoreType.DMA((2,))] * 2
        + [peers] * 4
        + [pltpu.SemaphoreType.DMA((3, CHUNKS, 2, half))] * 2
        + [pltpu.SemaphoreType.DMA((2, CHUNKS, 2, half))] * 2
        + [pltpu.SemaphoreType.DMA((3,))],
        compiler_params=pltpu.CompilerParams(
            collective_id=0, has_side_effects=True, vmem_limit_bytes=VMEM_LIMIT - held
        ),
    )(act, stash, cot, gain, *choices, *weights)


def store_kernel(count, *refs):
    sem = refs[2 * count]
    copies = [
        pltpu.make_async_copy(v.at[i], h.at[i], sem.at[n, i])
        for n, (v, h) in enumerate(zip(refs[:count], refs[count : 2 * count]))
        for i in range(v.shape[0])
    ]
    for copy in copies:
        copy.start()
    for copy in copies:
        copy.wait()


def store(arrays):
    count, most = len(arrays), max(a.shape[0] for a in arrays)
    return pl.pallas_call(
        functools.partial(store_kernel, count),
        out_shape=tuple(jax.ShapeDtypeStruct(a.shape, a.dtype) for a in arrays),
        in_specs=[ANY] * count,
        out_specs=(ANY,) * count,
        scratch_shapes=[pltpu.SemaphoreType.DMA((count, most))],
        compiler_params=pltpu.CompilerParams(vmem_limit_bytes=STORE_LIMIT),
    )(*(pltpu.with_memory_space_constraint(a, pltpu.VMEM) for a in arrays))


def per_device(
    sent_acts,
    stash,
    cotangents,
    norm_gain,
    w_gate,
    w_up,
    w_down,
    routes_next,
    gates_next,
    routes_prev,
    gates_prev,
):
    choices = [jnp.swapaxes(a[0], 0, 1) for a in (routes_next, gates_next, routes_prev, gates_prev)]
    fwd, bwd, gate_grad, *grads = tick_call(
        lax.axis_size("section"), lax.axis_size("expert"),
        sent_acts[0], stash[0], cotangents[0], norm_gain, choices, (w_gate[0], w_up[0], w_down[0]),
    )
    fwd, bwd, gate_grad, *grads = store((fwd[None], bwd[None], gate_grad[None], *grads))
    return (fwd, bwd, jnp.swapaxes(gate_grad, 1, 2)) + tuple(g[None] for g in grads)


def solution(mesh):
    tokens = P("section", "expert", None)
    weights = P("section", "expert", None, None)
    return jax.shard_map(
        per_device,
        mesh=mesh,
        in_specs=(tokens, tokens, tokens, P("section", None), weights, weights, weights)
        + (tokens,) * 4,
        out_specs=(tokens, tokens, tokens, weights, weights, weights),
        check_vma=False,
    )
```
